128 devices in a mesh: section: 4 (over z), space: 32 (over x, y, core).
Axes of the slice: x: 4, y: 4, z: 4, core: 2. Of those that a mesh axis runs over, the one named last changes fastest.
Arguments:
- features: bfloat16 [4, 128, 784, 256], P('section', 'space')
- tissue: int32 [4, 128], P('section'), may hold values from 0 to 1, as said below
- first_weight: bfloat16 [256, 512], replicated, may hold values from -0.375 to 0.375
- first_gain: float32 [512], replicated, may hold values from 0.1 to 1.9
- first_bias: float32 [512], replicated, may hold values from -3 to 3
- second_weight: bfloat16 [512, 1024], P(None, 'space'), may hold values from -0.25 to 0.25
- second_gain: float32 [1024], replicated, may hold values from 0.1 to 1.9
- second_bias: float32 [1024], replicated, may hold values from -3 to 3
Outputs:
- output: bfloat16 [4, 1024, 100352], P('section', 'space')
- first_mean: float32 [512], replicated
- first_var: float32 [512], replicated
- second_mean: float32 [1024], P('space')
- second_var: float32 [1024], P('space')
The draws below stay inside these ranges and needn't reach their ends.
Inputs may be any that keep to these rules, and one draw needn't show every extreme that they name: Every tile row holds at least one tissue tile and at least one tile without tissue.
All inputs are finite; a program needn't handle non-finite values.
Results may differ from the reference program's by a relative error of at most 0.0053.
Values may be sent and summed in bfloat16 or wider, within the bound.
No kernel may reach another device: no remote copies, remote signals or barrier semaphores. Data moves between devices by JAX's collectives and lax.ppermute only.
A program may use at most 128 MiB of HBM per device.

```python
import jax
import jax.numpy as jnp
from jax import lax

C1 = 256
C2 = 512
C3 = 1024
PIX = 784
MB = 4
TILES = 128


def draw_features(key, part):
    key_tile, key_chan, key_base = jax.random.split(key, 3)
    positions = jnp.arange(TILES).astype(jnp.float32) / max(TILES - 1, 1)
    tile_scale = jnp.power(10.0, positions)[None, :] * jnp.exp(jax.random.uniform(key_tile, (MB, TILES), jnp.float32, -0.35, 0.35))
    chan_scale = jnp.exp(jax.random.uniform(key_chan, (C1,), jnp.float32, -1.15, 1.15))
    base = jax.random.normal(key_base, (MB, TILES, PIX, C1), jnp.float32)
    values = base * tile_scale[:, :, None, None] * chan_scale
    return values.astype(jnp.bfloat16)


def draw_tissue(key, part):
    key_center, key_width, key_coin = jax.random.split(key, 3)
    center = jax.random.randint(key_center, (MB, 1), TILES // 5, 4 * TILES // 5 + 1)
    width = jax.random.randint(key_width, (MB, 1), TILES // 8 + 1, TILES // 3 + 1)
    places = jnp.arange(TILES)[None, :]
    coin = jax.random.randint(key_coin, (MB, TILES), 0, 10)
    inside = jnp.abs(places - center) < width
    mask = jnp.where(inside, (coin < 9).astype(jnp.int32), (coin < 1).astype(jnp.int32))
    mask = jnp.where(places == center, 1, mask)
    mask = jnp.where(places == (center + TILES // 2) % TILES, 0, mask)
    return mask.astype(jnp.int32)


def steps_of(stream_key, dims, cuts, least, high):
    def one(position, shards_of):
        heights = jax.random.uniform(jax.random.fold_in(jax.random.fold_in(stream_key, 6), position), (shards_of,), jnp.float32, least / len(cuts), high / len(cuts))
        return jnp.repeat(jnp.exp(heights), dims[position] // shards_of).reshape((-1,) + (1,) * (len(dims) - position - 1))

    level = one(*cuts[0])
    for cut in cuts[1:]:
        level = level * one(*cut)
    return level


def noise(key, extent, scale, limit, pieces=(), kind=jnp.bfloat16):
    drawn = scale * jax.random.normal(key, extent, jnp.float32)
    if pieces:
        drawn = drawn * steps_of(key, extent, pieces, -0.22, 0.18)
    return jnp.clip(drawn, -limit, limit).astype(kind)


def setup_inputs(seed: int = 0) -> dict:
    keys = jax.random.split(jax.random.key(seed), 9)
    return {
        "features": draw_features(jax.random.fold_in(keys[8], 71), 0),
        "tissue": draw_tissue(jax.random.fold_in(keys[8], 71), 0),
        "first_weight": noise(keys[2], (C1, C2), C1 ** -0.5, 0.375),
        "first_gain": jnp.clip(1.0 + 0.18 * jax.random.normal(keys[3], (C2,), jnp.float32), 0.1, 1.9),
        "first_bias": noise(keys[4], (C2,), 0.5, 3.0, (), jnp.float32),
        "second_weight": noise(keys[5], (C2, C3), C2 ** -0.5, 0.25, ((1, 32),)),
        "second_gain": jnp.clip(1.0 + 0.18 * jax.random.normal(keys[6], (C3,), jnp.float32), 0.1, 1.9),
        "second_bias": noise(keys[7], (C3,), 0.5, 3.0, (), jnp.float32),
    }


EPS = 1e-05

def statistics(values, weight, count):
    mean_val = lax.optimization_barrier(jnp.sum(values * weight, axis=(0, 1, 2))) / count
    centred = values - mean_val
    var_val = lax.optimization_barrier(jnp.sum(weight * centred * centred, axis=(0, 1, 2))) / count
    return (mean_val, var_val)

def normalize(values, mean_val, var_val, gain, bias):
    return jnp.maximum(gain * (values - mean_val) * lax.rsqrt(var_val + EPS) + bias, 0.0)

def reference(features, tissue, first_weight, first_gain, first_bias, second_weight, second_gain, second_bias):
    weight = tissue.astype(jnp.float32)[:, :, None, None]
    count = jnp.sum(tissue).astype(jnp.float32) * PIX
    first = jnp.einsum('mtpc,cd->mtpd', features.astype(jnp.float32), first_weight.astype(jnp.float32), precision=lax.Precision.HIGHEST)
    first_mean, first_var = statistics(first, weight, count)
    activation = normalize(first, first_mean, first_var, first_gain, first_bias).astype(jnp.bfloat16)
    second = jnp.einsum('mtpc,cd->mtpd', activation.astype(jnp.float32), second_weight.astype(jnp.float32), precision=lax.Precision.HIGHEST)
    second_mean, second_var = statistics(second, weight, count)
    output = normalize(second, second_mean, second_var, second_gain, second_bias).astype(jnp.bfloat16)
    output = jnp.transpose(output, (0, 3, 1, 2)).reshape(MB, C3, TILES * PIX)
    return (output, first_mean, first_var, second_mean, second_var)
```

```python
import jax
import jax.numpy as jnp
from jax import lax
from jax.sharding import Mesh
from jax.sharding import PartitionSpec as P

EPS = 1e-05
EVERY = ("z", "x", "y", "c")
PLANE = ("x", "y", "c")


def all_sum(values, axes):
    for axis in axes:
        values = lax.psum(values, (axis,))
    return values


def shards(
    features, tissue, first_weight, first_gain, first_bias, second_weight, second_gain, second_bias
):
    index = lax.axis_index(PLANE)
    tiles_here, pixels, depth = features.shape[1:]
    rows = features.reshape(tiles_here * pixels, depth)
    row_mask = tissue[0].astype(jnp.float32)
    own_mask = lax.dynamic_slice_in_dim(row_mask, index * tiles_here, tiles_here)
    own_weight = jnp.repeat(own_mask, pixels)
    first = jnp.dot(rows, first_weight, preferred_element_type=jnp.float32)
    total, count = all_sum(
        (jnp.sum(first * own_weight[:, None], axis=0), jnp.sum(own_mask) * pixels), EVERY
    )
    first_mean = total / count
    centred = first - first_mean
    first_var = all_sum(jnp.sum(own_weight[:, None] * centred * centred, axis=0), EVERY) / count
    activation = jnp.maximum(
        first_gain * centred * lax.rsqrt(first_var + EPS) + first_bias, 0.0
    ).astype(jnp.bfloat16)
    weights = lax.all_gather(second_weight, PLANE, axis=1, tiled=True)
    second = lax.dot_general(
        weights, activation, (((0,), (1,)), ((), ())), preferred_element_type=jnp.float32
    )
    centre = jnp.mean(second, axis=1)
    shifted = second - centre[:, None]
    tissue_sum = jnp.sum(shifted * own_weight, axis=1)
    tissue_squares = jnp.sum(shifted * shifted * own_weight, axis=1)
    width = second_weight.shape[1]
    moved = lax.all_to_all(
        shifted.astype(jnp.bfloat16).reshape(-1, width, tiles_here * pixels),
        PLANE,
        split_axis=0,
        concat_axis=0,
        tiled=True,
    )
    parts = lax.all_to_all(
        jnp.stack([centre, tissue_sum, tissue_squares], axis=1).reshape(-1, width, 3),
        PLANE,
        split_axis=0,
        concat_axis=0,
        tiled=True,
    )
    centres, sums, squares = parts[..., 0], parts[..., 1], parts[..., 2]
    held = (jnp.sum(row_mask.reshape(-1, tiles_here), axis=1) * pixels)[:, None]
    second_mean = all_sum(jnp.sum(sums + held * centres, axis=0), ("z",)) / count
    offset = centres - second_mean
    second_var = (
        all_sum(
            jnp.sum(squares + 2.0 * offset * sums + held * offset * offset, axis=0), ("z",)
        )
        / count
    )
    gain_here = lax.dynamic_slice_in_dim(second_gain, index * width, width)
    bias_here = lax.dynamic_slice_in_dim(second_bias, index * width, width)
    scale = gain_here * lax.rsqrt(second_var + EPS)
    output = jnp.maximum(
        (moved.astype(jnp.float32) + offset[..., None]) * scale[:, None] + bias_here[:, None], 0.0
    ).astype(jnp.bfloat16)
    output = jnp.transpose(output, (1, 0, 2)).reshape(1, width, -1)
    return (output, first_mean, first_var, second_mean, second_var)


def solution(mesh):
    fine = Mesh(mesh.devices.reshape(4, 4, 4, 2), EVERY)
    in_specs = (
        P("z", PLANE, None, None),
        P("z", None),
        P(),
        P(),
        P(),
        P(None, PLANE),
        P(),
        P(),
    )
    out_specs = (P("z", PLANE, None), P(), P(), P(PLANE), P(PLANE))
    return jax.shard_map(shards, mesh=fine, in_specs=in_specs, out_specs=out_specs, check_vma=False)
```

```python
import jax
import jax.numpy as jnp
from jax import lax
from jax.experimental import pallas as pl
from jax.experimental.pallas import tpu as pltpu
from jax.sharding import Mesh
from jax.sharding import PartitionSpec as P

EPS = 1e-05
EVERY = ("z", "x", "y", "c")
PLANE = ("x", "y", "c")
RING = 4
BAND = 128
HALF = BAND // 2


def place(x, y, c):
    return ((x % RING) * RING + y % RING) * 2 + c


def along(step, core0_axis, flip):
    pairs = []
    for x in range(RING):
        for y in range(RING):
            for c in range(2):
                on_x = (core0_axis == "x") == (c == 0)
                there = (x + step, y) if on_x else (x, y + step)
                pairs.append((place(x, y, c), place(*there, c ^ flip)))
    return pairs


def gather_step(values, step):
    return lax.ppermute(values, PLANE, along(step, "x", 0))


def exchange_step(values, step, flip):
    return lax.ppermute(values, PLANE, along(step, "y", flip))


def first_kernel(held_ref, rows_ref, weight_ref, out_ref):
    step = pl.program_id(0)
    first = jnp.dot(rows_ref[...], weight_ref[...], preferred_element_type=jnp.float32)

    @pl.when(step == 0)
    def _():
        out_ref[...] = jnp.zeros_like(out_ref)
        out_ref[0:1, :] = jnp.mean(first, axis=0, keepdims=True)

    centred = first - out_ref[0:1, :]
    held = held_ref[step].astype(jnp.float32)
    out_ref[1:2, :] += held * jnp.sum(centred, axis=0, keepdims=True)
    out_ref[2:3, :] += held * jnp.sum(centred * centred, axis=0, keepdims=True)


def first_sums(held, rows, weight):
    tiles, pixels, depth = rows.shape
    width = weight.shape[1]
    return pl.pallas_call(
        first_kernel,
        out_shape=jax.ShapeDtypeStruct((8, width), jnp.float32),
        grid_spec=pltpu.PrefetchScalarGridSpec(
            num_scalar_prefetch=1,
            grid=(tiles,),
            in_specs=[
                pl.BlockSpec((None, pixels, depth), lambda i, h: (i, 0, 0)),
                pl.BlockSpec((depth, width), lambda i, h: (0, 0)),
            ],
            out_specs=pl.BlockSpec((8, width), lambda i, h: (0, 0)),
        ),
        compiler_params=pltpu.CompilerParams(dimension_semantics=("arbitrary",)),
        name="first_sums",
    )(held, rows, weight)


def make_second_kernel(cuts, pixels, tiles, lanes, pieces, has_centre):
    n_in = sum(len(c) for c in cuts)
    slots = len(cuts)
    tile = lanes // pieces

    def kernel(core_ref, held_ref, *refs):
        inputs = refs[:n_in]
        w1_ref, mean_ref, scale_ref, bias_ref, w2_ref = refs[n_in : n_in + 5]
        rest = refs[n_in + 5 :]
        if has_centre:
            centre_ref, rest = rest[0], rest[1:]
        outs, stats_ref, rows, sems = rest[:8], rest[8], rest[9], rest[10]
        shift = pl.multiple_of(core_ref[0] * HALF, HALF)

        def copies(slot):
            first_input = sum(len(c) for c in cuts[:slot])
            return [
                pltpu.make_async_copy(
                    inputs[first_input + i],
                    rows.at[slot, pl.ds(pl.multiple_of(shift + start, 16), size), :],
                    sems.at[first_input + i],
                )
                for i, (start, size) in enumerate(cuts[slot])
            ]

        for slot in range(slots):
            for copy in copies(slot):
                copy.start()
            rest_at = pl.multiple_of((1 - core_ref[0]) * (lanes - HALF), HALF)
            rows[slot, pl.ds(rest_at, HALF), :] = jnp.zeros((HALF, rows.shape[2]), rows.dtype)
        width = outs[0].shape[1]
        wide = lambda v: jnp.concatenate([v] * (tile // BAND), axis=1)
        centre = centre_ref[...] if has_centre else None
        sums = squares = None
        for slot in range(slots):
            for copy in copies(slot):
                copy.wait()
            for piece in range(pieces):
                at = piece * tile
                block = rows[slot, at : at + tile, :]
                first = lax.dot_general(
                    w1_ref[...],
                    block,
                    (((1,), (1,)), ((), ())),
                    preferred_element_type=jnp.float32,
                )
                activation = jnp.maximum(
                    (first - wide(mean_ref[...])) * wide(scale_ref[...]) + wide(bias_ref[...]), 0.0
                ).astype(jnp.bfloat16)
                second = jnp.dot(w2_ref[...], activation, preferred_element_type=jnp.float32)
                if centre is None:
                    centre = jnp.broadcast_to(
                        jnp.mean(second[:, BAND:], axis=1, keepdims=True), (8 * width, BAND)
                    )
                second = second - wide(centre)
                lane = lax.broadcasted_iota(jnp.int32, (1, tile), 1) + (at - shift)
                held = jnp.zeros((1, tile), jnp.float32)
                for t in range(tiles):
                    inside = (lane >= t * pixels) & (lane < (t + 1) * pixels)
                    held += jnp.where(
                        inside, held_ref[slot * tiles + t].astype(jnp.float32), 0.0
                    )
                kept = second * held
                squared = kept * second
                part = sum(
                    kept[:, i * BAND : (i + 1) * BAND] for i in range(tile // BAND)
                )
                part2 = sum(
                    squared[:, i * BAND : (i + 1) * BAND] for i in range(tile // BAND)
                )
                sums = part if sums is None else sums + part
                squares = part2 if squares is None else squares + part2
                rounded = second.astype(jnp.bfloat16)
                for i in range(8):
                    outs[i][slot, :, at : at + tile] = rounded[i * width : (i + 1) * width, :]
        lane = lax.broadcasted_iota(jnp.int32, stats_ref.shape, 1)
        stats_ref[...] = jnp.where(
            lane == 0,
            centre,
            jnp.where(
                lane == 1,
                jnp.sum(sums, axis=1, keepdims=True),
                jnp.sum(squares, axis=1, keepdims=True),
            ),
        )

    return kernel


def second_values(core, held, groups, w1t, mean, scale, bias, w2t, centre, pixels, tiles):
    cuts, inputs = [], []
    for blocks in groups:
        start, cut = 0, []
        for block in blocks:
            cut.append((start, block.shape[0]))
            inputs.append(block)
            start += block.shape[0]
        cuts.append(tuple(cut))
    depth = w1t.shape[1]
    lanes = pixels * tiles + HALF
    width = w2t.shape[0] // 8
    pieces = 5
    vmem = pl.BlockSpec(memory_space=pltpu.VMEM)
    smem = pl.BlockSpec(memory_space=pltpu.SMEM)
    extra = [] if centre is None else [centre]
    outs = pl.pallas_call(
        make_second_kernel(tuple(cuts), pixels, tiles, lanes, pieces, centre is not None),
        out_shape=[jax.ShapeDtypeStruct((len(groups), width, lanes), jnp.bfloat16)] * 8
        + [jax.ShapeDtypeStruct((8 * width, BAND), jnp.float32)],
        in_specs=[smem, smem]
        + [pl.BlockSpec(memory_space=pl.ANY)] * len(inputs)
        + [vmem] * (5 + len(extra)),
        out_specs=[vmem] * 9,
        scratch_shapes=[
            pltpu.VMEM((len(groups), lanes, depth), jnp.bfloat16),
            pltpu.SemaphoreType.DMA((len(inputs),)),
        ],
        name="second_values",
    )(core, held, *inputs, w1t, mean, scale, bias, w2t, *extra)
    return outs[:8], outs[8]


def make_last_kernel(lanes, chip_lanes):
    cut = chip_lanes // 2 // BAND * BAND

    def kernel(spot_ref, *refs):
        moved = refs[:16]
        offset_ref, scale_ref, bias_ref, out_ref, inbuf, outbuf, in_sems, out_sems = refs[16:]
        core = spot_ref[2]

        def piece(ring, slot, flip):
            group, row = ((0, 0), (0, 1), (1, 1), (1, 0))[slot]
            return moved[group * 8 + ring * 2 + flip].at[row]

        def loads(a, b, c):
            n = a * RING + b
            return (
                pltpu.make_async_copy(piece(b, a, c), inbuf.at[n, 0], in_sems.at[n, 0]),
                pltpu.make_async_copy(piece(a, b, 1 - c), inbuf.at[n, 1], in_sems.at[n, 1]),
            )

        def store(a, b):
            n = a * RING + b
            chip = ((spot_ref[0] + RING - a) % RING) * RING + (spot_ref[1] + RING - b) % RING
            return pltpu.make_async_copy(
                outbuf.at[n],
                out_ref.at[:, pl.ds(pl.multiple_of(chip * chip_lanes, BAND), chip_lanes)],
                out_sems.at[n],
            )

        steps = [(a, b) for a in range(RING) for b in range(RING)]
        for a, b in steps:
            for c in range(2):

                @pl.when(core == c)
                def _():
                    for copy in loads(a, b, c):
                        copy.start()

        lane = lax.broadcasted_iota(jnp.int32, (1, BAND), 1)

        def finish(values, offset):
            wide = lambda v: jnp.concatenate([v] * (values.shape[1] // BAND), axis=1)
            return jnp.maximum(
                (values.astype(jnp.float32) + wide(offset)) * wide(scale_ref[...])
                + wide(bias_ref[...]),
                0.0,
            )

        for a, b in steps:
            n = a * RING + b
            for c in range(2):

                @pl.when(core == c)
                def _():
                    for copy in loads(a, b, c):
                        copy.wait()

            left_offset = offset_ref[b * 2 + core]
            right_offset = offset_ref[a * 2 + 1 - core]
            left = inbuf.at[n, 0]
            right = inbuf.at[n, 1]
            outbuf[n, :, :cut] = finish(left[:, :cut], left_offset).astype(jnp.bfloat16)
            middle = jnp.where(
                lane < HALF,
                finish(left[:, cut : cut + BAND], left_offset),
                finish(right[:, :BAND], right_offset),
            )
            outbuf[n, :, cut : cut + BAND] = middle.astype(jnp.bfloat16)
            outbuf[n, :, cut + BAND :] = finish(right[:, BAND:], right_offset).astype(jnp.bfloat16)
            store(a, b).start()
        for a, b in steps:
            store(a, b).wait()

    return kernel


def last_pass(spot, moved, offsets, scale, bias, chip_lanes):
    slots, width, lanes = moved[0].shape
    vmem = pl.BlockSpec(memory_space=pltpu.VMEM)
    anywhere = pl.BlockSpec(memory_space=pl.ANY)
    chips = RING * RING
    return pl.pallas_call(
        make_last_kernel(lanes, chip_lanes),
        out_shape=jax.ShapeDtypeStruct((width, chips * chip_lanes), jnp.bfloat16),
        in_specs=[pl.BlockSpec(memory_space=pltpu.SMEM)] + [anywhere] * 16 + [vmem] * 3,
        out_specs=anywhere,
        scratch_shapes=[
            pltpu.VMEM((chips, 2, width, lanes), jnp.bfloat16),
            pltpu.VMEM((chips, width, chip_lanes), jnp.bfloat16),
            pltpu.SemaphoreType.DMA((chips, 2)),
            pltpu.SemaphoreType.DMA((chips,)),
        ],
        name="last_pass",
    )(spot, *moved, offsets, scale, bias)


def merge(counts, means, squares):
    total = jnp.sum(counts, axis=0)
    safe = jnp.maximum(total, 1.0)
    centre = means[0]
    mean_val = centre + jnp.sum(counts * (means - centre), axis=0) / safe
    spread = jnp.sum(squares + counts * (means - mean_val) ** 2, axis=0)
    return total, mean_val, spread


def share(counts, means, squares, axes):
    members = 1
    for axis in axes:
        members *= lax.axis_size(axis)
    width = means.shape[0]
    message = jnp.concatenate([counts, means, squares])
    everyone = lax.all_to_all(
        jnp.broadcast_to(message[None], (members, 3 * width)),
        axes,
        split_axis=0,
        concat_axis=0,
        tiled=True,
    )
    return merge(everyone[:, :width], everyone[:, width : 2 * width], everyone[:, 2 * width :])


def local_moments(count, centre, sums, squares):
    safe = jnp.maximum(count, 1.0)
    return centre + sums / safe, squares - sums * sums / safe


def band(values):
    return jnp.broadcast_to(values[..., None], values.shape + (BAND,))


def shards(
    features, tissue, first_weight, first_gain, first_bias, second_weight, second_gain, second_bias
):
    x, y, c = (lax.axis_index(axis) for axis in PLANE)
    index = lax.axis_index(PLANE)
    tiles, pixels, depth = features.shape[1:]
    rows = features.reshape(tiles * pixels, depth)
    row_tissue = tissue[0]
    tissue_rows = row_tissue.reshape(-1, tiles)
    half = tiles * pixels // 2

    ahead = gather_step(rows, 1)
    behind = gather_step(rows, 3)
    slice_here = second_weight.T
    pair = jnp.concatenate(
        [slice_here, lax.ppermute(slice_here, "c", [(0, 1), (1, 0)])], axis=0
    )
    pairs = [pair] + [exchange_step(pair, step, 0) for step in (3, 2, 1)]
    w2t = jnp.concatenate(pairs, axis=0)

    held_here = lax.dynamic_slice_in_dim(row_tissue, index * tiles, tiles)
    sums = first_sums(held_here, features[0], first_weight)
    held_count = (jnp.sum(held_here) * pixels).astype(jnp.float32)
    mean_here, spread_here = local_moments(held_count, sums[0], sums[1], sums[2])
    moments = (jnp.full_like(mean_here, held_count), mean_here, spread_here)
    moments = share(*moments, ("z", "c"))
    counts, first_mean, spread = share(*moments, ("x", "y"))
    first_var = spread / counts
    count = counts[0]
    first_scale = first_gain * lax.rsqrt(first_var + EPS)

    far = (gather_step(ahead[:half], 1), gather_step(behind[half:], 3))

    core = c.reshape(1)
    w1t = first_weight.T
    steps = jnp.arange(RING)
    ring_rows = jnp.where(
        c == 0, place((x - steps) % RING, y, 0), place(x, (y - steps) % RING, 1)
    )
    ring_tissue = jnp.take(tissue_rows, ring_rows, axis=0)
    held_near = ring_tissue[:2].reshape(-1)
    held_far = jnp.stack([ring_tissue[3], ring_tissue[2]]).reshape(-1)
    norm = (w1t, band(first_mean), band(first_scale), band(first_bias), w2t)
    near, near_stats = second_values(
        core, held_near, [[rows], [ahead]], *norm, None, pixels, tiles
    )
    centre = band(near_stats[:, 0])
    routes = [(step, flip) for step in range(RING) for flip in range(2)]

    def send(blocks):
        return [
            block if route == (0, 0) else exchange_step(block, *route)
            for route, block in zip(routes, blocks)
        ]

    moved_near = send(near)
    rest, rest_stats = second_values(
        core, held_far, [[behind], list(far)], *norm, centre, pixels, tiles
    )
    moved_rest = send(rest)

    ring_count = (jnp.sum(ring_tissue) * pixels).astype(jnp.float32)
    mean_here, spread_here = local_moments(
        ring_count,
        near_stats[:, 0],
        near_stats[:, 1] + rest_stats[:, 1],
        near_stats[:, 2] + rest_stats[:, 2],
    )
    merged = share(jnp.full_like(mean_here, ring_count), mean_here, spread_here, ("z",))
    letters = jnp.stack([*merged, near_stats[:, 0]]).reshape(4, 8, -1)
    arrived = jnp.stack(send([letters[:, i] for i in range(8)]))
    _, second_mean, spread = merge(arrived[:, 0], arrived[:, 1], arrived[:, 2])
    second_var = spread / count
    width = second_weight.shape[1]
    gain_here = lax.dynamic_slice_in_dim(second_gain, index * width, width)
    bias_here = lax.dynamic_slice_in_dim(second_bias, index * width, width)
    scale = gain_here * lax.rsqrt(second_var + EPS)
    output = last_pass(
        jnp.stack([x, y, c]),
        moved_near + moved_rest,
        band(arrived[:, 3] - second_mean),
        band(scale),
        band(bias_here),
        2 * tiles * pixels,
    )
    return (output[None], first_mean, first_var, second_mean, second_var)


def solution(mesh):
    fine = Mesh(mesh.devices.reshape(RING, RING, RING, 2), EVERY)
    in_specs = (
        P("z", PLANE, None, None),
        P("z", None),
        P(),
        P(),
        P(),
        P(None, PLANE),
        P(),
        P(),
    )
    out_specs = (P("z", PLANE, None), P(), P(), P(PLANE), P(PLANE))
    return jax.shard_map(shards, mesh=fine, in_specs=in_specs, out_specs=out_specs, check_vma=False)
```

```python
import jax
import jax.numpy as jnp
from jax import lax
from jax.experimental import pallas as pl
from jax.experimental.pallas import tpu as pltpu
from jax.sharding import Mesh
from jax.sharding import PartitionSpec as P


EPS = 1e-05
EVERY = ("z", "x", "y", "c")
PLANE = ("x", "y", "c")
RING = 4
BAND = 128
HALF = BAND // 2
PIECE = 512


def place(x, y, c):
    return ((x % RING) * RING + y % RING) * 2 + c


def along(step, core0_axis, flip):
    pairs = []
    for x in range(RING):
        for y in range(RING):
            for c in range(2):
                on_x = (core0_axis == "x") == (c == 0)
                there = (x + step, y) if on_x else (x, y + step)
                pairs.append((place(x, y, c), place(*there, c ^ flip)))
    return pairs


def gather_step(values, step):
    return lax.ppermute(values, PLANE, along(step, "x", 0))


def exchange_step(values, step, flip):
    return lax.ppermute(values, PLANE, along(step, "y", flip))


def spot():
    return tuple(lax.axis_index(axis) for axis in PLANE)


def tissue_of(tissue_ref, chip_x, chip_y, core, tiles):
    base = place(chip_x, chip_y, core) * tiles
    return [tissue_ref[base + t].astype(jnp.float32) for t in range(tiles)]


def ring_spot(slot):
    x, y, c = spot()
    along_x, along_y = (1 - c) * slot, c * slot
    return (x + RING - along_x) % RING, (y + RING - along_y) % RING, c


def merge(counts, means, squares):
    total = jnp.sum(counts, axis=0)
    centre = means[0]
    mean_val = centre + jnp.sum(counts * (means - centre), axis=0) / jnp.maximum(total, 1.0)
    spread = jnp.sum(squares + counts * (means - mean_val) ** 2, axis=0)
    return total, mean_val, spread


def local_moments(count, centre, sums, squares):
    safe = jnp.maximum(count, 1.0)
    return centre + sums / safe, squares - sums * sums / safe


def first_kernel(tissue_ref, rows_ref, weight_ref, own_ref, mate_ref, out_ref, turned_ref, pair_ref, acc_ref):
    step = pl.program_id(0)
    tiles = pl.num_programs(0)
    pixels = rows_ref.shape[0]
    base = place(*spot()) * tiles
    first = jnp.dot(rows_ref[...], weight_ref[...], preferred_element_type=jnp.float32)

    @pl.when(step == 0)
    def _():
        acc_ref[...] = jnp.zeros_like(acc_ref)
        acc_ref[0:1, :] = jnp.mean(first, axis=0, keepdims=True)
        turned_ref[...] = weight_ref[...].T
        width = own_ref.shape[0]
        pair_ref[:width, :] = own_ref[...]
        pair_ref[width:, :] = mate_ref[...]

    centred = first - acc_ref[0:1, :]
    held = tissue_ref[base + step].astype(jnp.float32)
    acc_ref[1:2, :] += held * jnp.sum(centred, axis=0, keepdims=True)
    acc_ref[2:3, :] += held * jnp.sum(centred * centred, axis=0, keepdims=True)
    acc_ref[3:4, :] += jnp.full((1, acc_ref.shape[1]), held * pixels, jnp.float32)

    @pl.when(step == tiles - 1)
    def _():
        count = acc_ref[3:4, :]
        mean, spread = local_moments(count, acc_ref[0:1, :], acc_ref[1:2, :], acc_ref[2:3, :])
        parts = acc_ref.shape[1] // BAND
        for r, row in enumerate((count, mean, spread)):
            for q in range(parts):
                out_ref[:, r * parts + q, :] = jnp.broadcast_to(
                    row[:, q * BAND : (q + 1) * BAND], (out_ref.shape[0], BAND)
                )


def first_sums(tissue, rows, weight, own, mate, members):
    tiles, pixels, depth = rows.shape
    width = weight.shape[1]
    whole = lambda shape: pl.BlockSpec(shape, lambda i, t: (0,) * len(shape))
    return pl.pallas_call(
        first_kernel,
        out_shape=[
            jax.ShapeDtypeStruct((members, 16, BAND), jnp.float32),
            jax.ShapeDtypeStruct((width, depth), jnp.bfloat16),
            jax.ShapeDtypeStruct((2 * own.shape[0], own.shape[1]), jnp.bfloat16),
        ],
        grid_spec=pltpu.PrefetchScalarGridSpec(
            num_scalar_prefetch=1,
            grid=(tiles,),
            in_specs=[
                pl.BlockSpec((None, pixels, depth), lambda i, t: (i, 0, 0)),
                whole(weight.shape),
                whole(own.shape),
                whole(mate.shape),
            ],
            out_specs=[
                whole((members, 16, BAND)),
                whole((width, depth)),
                whole((2 * own.shape[0], own.shape[1])),
            ],
            scratch_shapes=[pltpu.VMEM((8, width), jnp.float32)],
        ),
        compiler_params=pltpu.CompilerParams(dimension_semantics=("arbitrary",)),
        name="first_sums",
    )(tissue, rows, weight, own, mate)


def near_merge_kernel(in_ref, out_ref):
    parts = 4
    got = in_ref[...]
    rows = merge(*(got[:, r * parts : (r + 1) * parts, :] for r in range(3)))
    for r, row in enumerate(rows):
        out_ref[:, r * parts : (r + 1) * parts, :] = jnp.broadcast_to(
            row[None], (out_ref.shape[0], parts, BAND)
        )


def near_merge(messages, members):
    return pl.pallas_call(
        near_merge_kernel,
        out_shape=jax.ShapeDtypeStruct((members, 16, BAND), jnp.float32),
        name="near_merge",
    )(messages)


def whole_merge_kernel(in_ref, gain_ref, bias_ref, mean_ref, var_ref, mean_col, scale_col, bias_col):
    parts = mean_ref.shape[0]
    got = in_ref[...]
    count, mean, spread = merge(*(got[:, r * parts : (r + 1) * parts, :] for r in range(3)))
    var = spread / count
    mean_ref[...] = mean
    var_ref[...] = var
    for value, col in (
        (mean, mean_col),
        (gain_ref[...] * lax.rsqrt(var + EPS), scale_col),
        (bias_ref[...], bias_col),
    ):
        for q in range(parts):
            col[q * BAND : (q + 1) * BAND, :] = jnp.broadcast_to(value[q : q + 1, :], (BAND, BAND)).T


def whole_merge(messages, gain, bias):
    width = gain.shape[0]
    row = jax.ShapeDtypeStruct((width // BAND, BAND), jnp.float32)
    col = jax.ShapeDtypeStruct((width, BAND), jnp.float32)
    return pl.pallas_call(
        whole_merge_kernel, out_shape=[row, row, col, col, col], name="whole_merge"
    )(messages, gain.reshape(row.shape), bias.reshape(row.shape))


def make_second_kernel(cuts, order, pixels, tiles, lanes, last):
    n_in = sum(len(c) for c in cuts)
    slots = len(cuts)

    def kernel(tissue_ref, *refs):
        inputs = refs[:n_in]
        w1_ref, mean_ref, scale_ref, bias_ref = refs[n_in : n_in + 4]
        w2_refs = refs[n_in + 4 : n_in + 8]
        rest = refs[n_in + 8 :]
        if last:
            before_ref, rest = rest[0], rest[1:]
        outs, stats_ref, rows, w2_ref, sems = rest[:8], rest[8], rest[9], rest[10], rest[11]
        core = lax.axis_index("c")
        shift = pl.multiple_of(core * HALF, HALF)

        def copies(slot):
            first_input = sum(len(c) for c in cuts[:slot])
            return [
                pltpu.make_async_copy(
                    inputs[first_input + i],
                    rows.at[slot, pl.ds(pl.multiple_of(shift + start, 16), size), :],
                    sems.at[first_input + i],
                )
                for i, (start, size) in enumerate(cuts[slot])
            ]

        for slot in range(slots):
            for copy in copies(slot):
                copy.start()
            rest_at = pl.multiple_of((1 - core) * (lanes - HALF), HALF)
            rows[slot, pl.ds(rest_at, HALF), :] = jnp.zeros((HALF, rows.shape[2]), rows.dtype)
        for i, ref in enumerate(w2_refs):
            w2_ref[i * ref.shape[0] : (i + 1) * ref.shape[0], :] = ref[...]
        width = outs[0].shape[1]
        centre = jnp.broadcast_to(before_ref[:, 0:1], (8 * width, BAND)) if last else None
        sums = squares = None
        for slot in range(slots):
            held_here = tissue_of(tissue_ref, *ring_spot(order[slot]), tiles)
            for copy in copies(slot):
                copy.wait()
            for at in range(0, lanes, PIECE):
                tile = min(PIECE, lanes - at)
                wide = lambda v: jnp.concatenate([v] * (tile // BAND), axis=1)
                block = rows[slot, at : at + tile, :]
                first = lax.dot_general(
                    w1_ref[...],
                    block,
                    (((1,), (1,)), ((), ())),
                    preferred_element_type=jnp.float32,
                )
                activation = jnp.maximum(
                    (first - wide(mean_ref[...])) * wide(scale_ref[...]) + wide(bias_ref[...]), 0.0
                ).astype(jnp.bfloat16)
                second = jnp.dot(w2_ref[...], activation, preferred_element_type=jnp.float32)
                if centre is None:
                    centre = jnp.broadcast_to(
                        jnp.mean(second[:, BAND:], axis=1, keepdims=True), (8 * width, BAND)
                    )
                second = second - wide(centre)
                lane = lax.broadcasted_iota(jnp.int32, (1, tile), 1) + (at - shift)
                held = jnp.zeros((1, tile), jnp.float32)
                for t in range(tiles):
                    inside = (lane >= t * pixels) & (lane < (t + 1) * pixels)
                    held += jnp.where(inside, held_here[t], 0.0)
                kept = second * held
                squared = kept * second
                part = sum(kept[:, i * BAND : (i + 1) * BAND] for i in range(tile // BAND))
                part2 = sum(squared[:, i * BAND : (i + 1) * BAND] for i in range(tile // BAND))
                sums = part if sums is None else sums + part
                squares = part2 if squares is None else squares + part2
                rounded = second.astype(jnp.bfloat16)
                for i in range(8):
                    outs[i][slot, :, at : at + tile] = rounded[i * width : (i + 1) * width, :]
        lane = lax.broadcasted_iota(jnp.int32, (8 * width, BAND), 1)
        sums = jnp.sum(sums, axis=1, keepdims=True)
        squares = jnp.sum(squares, axis=1, keepdims=True)
        if last:
            count = sum(
                held for slot in range(RING) for held in tissue_of(tissue_ref, *ring_spot(slot), tiles)
            )
            count = jnp.full((8 * width, 1), count * pixels, jnp.float32)
            mean, spread = local_moments(
                count, before_ref[:, 0:1], before_ref[:, 1:2] + sums, before_ref[:, 2:3] + squares
            )
            message = jnp.where(lane == 0, count, jnp.where(lane == 1, mean, spread)).T[:8, :]
            stats_ref[...] = jnp.broadcast_to(message[None], stats_ref.shape)
        else:
            stats_ref[...] = jnp.where(lane == 0, centre, jnp.where(lane == 1, sums, squares))

    return kernel


def second_values(tissue, groups, order, norm, pairs, before, pixels, tiles):
    cuts, inputs = [], []
    for blocks in groups:
        start, cut = 0, []
        for block in blocks:
            cut.append((start, block.shape[0]))
            inputs.append(block)
            start += block.shape[0]
        cuts.append(tuple(cut))
    depth = norm[0].shape[1]
    lanes = pixels * tiles + HALF
    channels = sum(pair.shape[0] for pair in pairs)
    vmem = pl.BlockSpec(memory_space=pltpu.VMEM)
    extra = [] if before is None else [before]
    stats = (channels, BAND) if before is None else (RING, 8, channels)
    outs = pl.pallas_call(
        make_second_kernel(tuple(cuts), order, pixels, tiles, lanes, before is not None),
        out_shape=[jax.ShapeDtypeStruct((len(groups), channels // 8, lanes), jnp.bfloat16)] * 8
        + [jax.ShapeDtypeStruct(stats, jnp.float32)],
        in_specs=[pl.BlockSpec(memory_space=pltpu.SMEM)]
        + [pl.BlockSpec(memory_space=pl.ANY)] * len(inputs)
        + [vmem] * (8 + len(extra)),
        out_specs=[vmem] * 9,
        scratch_shapes=[
            pltpu.VMEM((len(groups), lanes, depth), jnp.bfloat16),
            pltpu.VMEM((channels, norm[0].shape[0]), jnp.bfloat16),
            pltpu.SemaphoreType.DMA((len(inputs),)),
        ],
        name="second_values",
    )(tissue, *inputs, *norm, *pairs, *extra)
    return outs[:8], outs[8]


def letters_kernel(in_ref, before_ref, *outs):
    got = in_ref[...]
    channels = got.shape[2]
    rows = merge(got[:, 0:1, :], got[:, 1:2, :], got[:, 2:3, :])
    stacked = jnp.concatenate([*rows, jnp.zeros((BAND - 3, channels), jnp.float32)], axis=0).T
    lane = lax.broadcasted_iota(jnp.int32, stacked.shape, 1)
    stacked = jnp.where(lane == 3, before_ref[:, 0:1], stacked)
    width = channels // 8
    for i, out in enumerate(outs):
        out[...] = stacked[i * width : (i + 1) * width, :]


def letters_of(messages, before):
    width = before.shape[0] // 8
    return pl.pallas_call(
        letters_kernel,
        out_shape=[jax.ShapeDtypeStruct((width, BAND), jnp.float32)] * 8,
        name="letters",
    )(messages, before)


def make_last_kernel(chip_lanes):
    cut = chip_lanes // 2 // BAND * BAND

    def kernel(*refs):
        moved, letters = refs[:16], refs[16:24]
        gain_ref, bias_ref, out_ref, mean_ref, var_ref = refs[24:29]
        inbuf, outbuf, offset_ref, in_sems, out_sems = refs[29:]
        x, y, core = spot()

        def piece(ring, slot, flip):
            group, row = ((0, 0), (0, 1), (1, 0), (0, 2))[slot]
            return moved[group * 8 + ring * 2 + flip].at[row]

        def loads(a, b, c):
            n = a * RING + b
            return (
                pltpu.make_async_copy(piece(b, a, c), inbuf.at[n, 0], in_sems.at[n, 0]),
                pltpu.make_async_copy(piece(a, b, 1 - c), inbuf.at[n, 1], in_sems.at[n, 1]),
            )

        def store(a, b):
            n = a * RING + b
            chip = ((x + RING - a) % RING) * RING + (y + RING - b) % RING
            return pltpu.make_async_copy(
                outbuf.at[n],
                out_ref.at[:, pl.ds(pl.multiple_of(chip * chip_lanes, BAND), chip_lanes)],
                out_sems.at[n],
            )

        steps = [(a, b) for a in range(RING) for b in range(RING)]
        for a, b in steps:
            for c in range(2):

                @pl.when(core == c)
                def _():
                    for copy in loads(a, b, c):
                        copy.start()

        width = letters[0].shape[0]
        got = jnp.stack([ref[...] for ref in letters])
        count, mean, spread = merge(got[:, :, 0:1], got[:, :, 1:2], got[:, :, 2:3])
        var = spread / count
        for i in range(8):
            offset_ref[i] = jnp.broadcast_to(got[i, :, 3:4] - mean, (width, BAND))
        lane = lax.broadcasted_iota(jnp.int32, (width, BAND), 1)
        row = lax.broadcasted_iota(jnp.int32, (width, BAND), 0)
        device = place(x, y, core)
        per_row = BAND // width

        def own_channels(ref):
            line = ref[pl.ds(device // per_row, 1), :]
            here = lane == row + (device % per_row) * width
            return jnp.sum(jnp.where(here, line, 0.0), axis=1, keepdims=True)

        scale = jnp.broadcast_to(own_channels(gain_ref) * lax.rsqrt(var + EPS), (width, BAND))
        bias = jnp.broadcast_to(own_channels(bias_ref), (width, BAND))
        for value, ref in ((mean, mean_ref), (var, var_ref)):
            line = jnp.sum(jnp.where(lane == row, value, 0.0), axis=0, keepdims=True)
            ref[...] = line[:, :width]

        def finish(values, offset):
            wide = lambda v: jnp.concatenate([v] * (values.shape[1] // BAND), axis=1)
            return jnp.maximum(
                (values.astype(jnp.float32) + wide(offset)) * wide(scale) + wide(bias), 0.0
            )

        for a, b in steps:
            n = a * RING + b
            for c in range(2):

                @pl.when(core == c)
                def _():
                    for copy in loads(a, b, c):
                        copy.wait()

            left_offset = offset_ref[b * 2 + core]
            right_offset = offset_ref[a * 2 + 1 - core]
            left = inbuf.at[n, 0]
            right = inbuf.at[n, 1]
            outbuf[n, :, :cut] = finish(left[:, :cut], left_offset).astype(jnp.bfloat16)
            middle = jnp.where(
                lane < HALF,
                finish(left[:, cut : cut + BAND], left_offset),
                finish(right[:, :BAND], right_offset),
            )
            outbuf[n, :, cut : cut + BAND] = middle.astype(jnp.bfloat16)
            outbuf[n, :, cut + BAND :] = finish(right[:, BAND:], right_offset).astype(jnp.bfloat16)
            store(a, b).start()
        for a, b in steps:
            store(a, b).wait()

    return kernel


def last_pass(moved, letters, gain, bias, chip_lanes):
    _, width, lanes = moved[0].shape
    vmem = pl.BlockSpec(memory_space=pltpu.VMEM)
    hbm = pl.BlockSpec(memory_space=pl.ANY)
    chips = RING * RING
    stat = jax.ShapeDtypeStruct((1, width), jnp.float32)
    return pl.pallas_call(
        make_last_kernel(chip_lanes),
        out_shape=[jax.ShapeDtypeStruct((width, chips * chip_lanes), jnp.bfloat16), stat, stat],
        in_specs=[hbm] * 16 + [vmem] * 10,
        out_specs=[hbm, vmem, vmem],
        scratch_shapes=[
            pltpu.VMEM((chips, 2, width, lanes), jnp.bfloat16),
            pltpu.VMEM((chips, width, chip_lanes), jnp.bfloat16),
            pltpu.VMEM((8, width, BAND), jnp.float32),
            pltpu.SemaphoreType.DMA((chips, 2)),
            pltpu.SemaphoreType.DMA((chips,)),
        ],
        name="last_pass",
    )(*moved, *letters, gain.reshape(-1, BAND), bias.reshape(-1, BAND))


def trade(messages, axes):
    return lax.all_to_all(messages, axes, split_axis=0, concat_axis=0, tiled=True)


ROUTES = [(step, flip) for step in range(RING) for flip in range(2)]


def send(blocks):
    return [
        block if route == (0, 0) else exchange_step(block, *route)
        for route, block in zip(ROUTES, blocks)
    ]


def shards(
    features, tissue, first_weight, first_gain, first_bias, second_weight, second_gain, second_bias
):
    tiles, pixels, depth = features.shape[1:]
    rows = features.reshape(tiles * pixels, depth)
    row_tissue = tissue[0]
    half = tiles * pixels // 2
    own = second_weight.T
    mate = lax.ppermute(own, "c", [(0, 1), (1, 0)])
    ahead = gather_step(rows, 1)
    behind = gather_step(rows, 3)
    messages, w1t, pair = first_sums(
        row_tissue, features[0], first_weight, own, mate, 2 * RING
    )
    pairs = [pair] + [exchange_step(pair, step, 0) for step in (3, 2, 1)]
    messages = trade(messages, ("z", "c"))
    messages, pairs = lax.optimization_barrier((messages, pairs))
    messages = near_merge(messages, RING * RING)
    messages = trade(messages, ("x", "y"))
    far = [gather_step(ahead[:half], 1), gather_step(behind[half:], 3)]
    first_mean, first_var, *norm = whole_merge(messages, first_gain, first_bias)
    near, before = second_values(
        row_tissue, [[rows], [ahead], [behind]], (0, 1, 3), (w1t, *norm), pairs, None, pixels, tiles
    )
    moved = send(near)
    rest, messages = second_values(
        row_tissue, [far], (2,), (w1t, *norm), pairs, before, pixels, tiles
    )
    moved += send(rest)
    messages = trade(messages, ("z",))
    letters = letters_of(messages, before)
    letters = send(letters)
    output, second_mean, second_var = last_pass(
        moved, letters, second_gain, second_bias, 2 * tiles * pixels
    )
    return (
        output[None],
        first_mean.reshape(-1),
        first_var.reshape(-1),
        second_mean[0],
        second_var[0],
    )


def solution(mesh):
    fine = Mesh(mesh.devices.reshape(RING, RING, RING, 2), EVERY)
    in_specs = (
        P("z", PLANE, None, None),
        P("z", None),
        P(),
        P(),
        P(),
        P(None, PLANE),
        P(),
        P(),
    )
    out_specs = (P("z", PLANE, None), P(), P(), P(PLANE), P(PLANE))
    return jax.shard_map(
        shards, mesh=fine, in_specs=in_specs, out_specs=out_specs, check_vma=False
    )
```

```python
import jax
import jax.numpy as jnp
from jax import lax
from jax.experimental import pallas as pl
from jax.experimental.pallas import tpu as pltpu
from jax.sharding import Mesh
from jax.sharding import PartitionSpec as P


EPS = 1e-05
EVERY = ("z", "x", "y", "c")
PLANE = ("x", "y", "c")
RING = 4
MIB = 1 << 20
BAND = 128
HALF = BAND // 2
PIECE = 512


def place(x, y, c):
    return ((x % RING) * RING + y % RING) * 2 + c


def along(step, core0_axis, flip):
    pairs = []
    for x in range(RING):
        for y in range(RING):
            for c in range(2):
                on_x = (core0_axis == "x") == (c == 0)
                there = (x + step, y) if on_x else (x, y + step)
                pairs.append((place(x, y, c), place(*there, c ^ flip)))
    return pairs


def gather_step(values, step):
    return lax.ppermute(values, PLANE, along(step, "x", 0))


def exchange_step(values, step, flip):
    return lax.ppermute(values, PLANE, along(step, "y", flip))


def spot():
    return tuple(lax.axis_index(axis) for axis in PLANE)


def tissue_of(tissue_ref, chip_x, chip_y, core, tiles):
    base = place(chip_x, chip_y, core) * tiles
    return [tissue_ref[base + t].astype(jnp.float32) for t in range(tiles)]


def ring_spot(slot):
    x, y, c = spot()
    along_x, along_y = (1 - c) * slot, c * slot
    return (x + RING - along_x) % RING, (y + RING - along_y) % RING, c


def merge(counts, means, squares):
    total = jnp.sum(counts, axis=0)
    centre = means[0]
    mean_val = centre + jnp.sum(counts * (means - centre), axis=0) / jnp.maximum(total, 1.0)
    spread = jnp.sum(squares + counts * (means - mean_val) ** 2, axis=0)
    return total, mean_val, spread


def local_moments(count, centre, sums, squares):
    safe = jnp.maximum(count, 1.0)
    return centre + sums / safe, squares - sums * sums / safe


def first_kernel(tissue_ref, rows_ref, weight_ref, own_ref, mate_ref, out_ref, turned_ref, pair_ref, acc_ref):
    step = pl.program_id(0)
    tiles = pl.num_programs(0)
    pixels = rows_ref.shape[0]
    width = weight_ref.shape[1]
    base = place(*spot()) * tiles
    held = tissue_ref[base + step].astype(jnp.float32)
    chunk = pixels // 7

    def part(i):
        return jnp.dot(
            rows_ref[i * chunk : (i + 1) * chunk, :],
            weight_ref[...],
            preferred_element_type=jnp.float32,
        )

    @pl.when(step == 0)
    def _():
        acc_ref[...] = jnp.zeros_like(acc_ref)
        acc_ref[0] = jnp.broadcast_to(jnp.mean(part(0), axis=0, keepdims=True), (8, width))
        turned_ref[...] = weight_ref[...].T
        half = own_ref.shape[0]
        pair_ref[:half, :] = own_ref[...]
        pair_ref[half:, :] = mate_ref[...]

    centre = acc_ref[0]
    sums = jnp.zeros((8, width), jnp.float32)
    squares = jnp.zeros((8, width), jnp.float32)
    for i in range(7):
        centred = part(i).reshape(chunk // 8, 8, width) - centre
        sums += jnp.sum(centred, axis=0)
        squares += jnp.sum(centred * centred, axis=0)
    acc_ref[1] += held * sums
    acc_ref[2] += held * squares
    acc_ref[3] += jnp.full((8, width), held * pixels, jnp.float32)

    @pl.when(step == tiles - 1)
    def _():
        count = acc_ref[3, 0:1, :]
        mean, spread = local_moments(
            count,
            acc_ref[0, 0:1, :],
            jnp.sum(acc_ref[1], axis=0, keepdims=True),
            jnp.sum(acc_ref[2], axis=0, keepdims=True),
        )
        parts = width // BAND
        for r, row in enumerate((count, mean, spread)):
            for q in range(parts):
                out_ref[:, r * parts + q, :] = jnp.broadcast_to(
                    row[:, q * BAND : (q + 1) * BAND], (out_ref.shape[0], BAND)
                )


def first_sums(tissue, rows, weight, own, mate, members):
    tiles, pixels, depth = rows.shape
    width = weight.shape[1]
    whole = lambda shape: pl.BlockSpec(shape, lambda i, t: (0,) * len(shape))
    return pl.pallas_call(
        first_kernel,
        out_shape=[
            jax.ShapeDtypeStruct((members, 16, BAND), jnp.float32),
            jax.ShapeDtypeStruct((width, depth), jnp.bfloat16),
            jax.ShapeDtypeStruct((2 * own.shape[0], own.shape[1]), jnp.bfloat16),
        ],
        grid_spec=pltpu.PrefetchScalarGridSpec(
            num_scalar_prefetch=1,
            grid=(tiles,),
            in_specs=[
                pl.BlockSpec((None, pixels, depth), lambda i, t: (i, 0, 0)),
                whole(weight.shape),
                whole(own.shape),
                whole(mate.shape),
            ],
            out_specs=[
                whole((members, 16, BAND)),
                whole((width, depth)),
                whole((2 * own.shape[0], own.shape[1])),
            ],
            scratch_shapes=[pltpu.VMEM((4, 8, width), jnp.float32)],
        ),
        compiler_params=pltpu.CompilerParams(dimension_semantics=("arbitrary",)),
        name="first_sums",
    )(tissue, rows, weight, own, mate)


def near_merge_kernel(in_ref, out_ref):
    parts = 4
    got = in_ref[...]
    rows = merge(*(got[:, r * parts : (r + 1) * parts, :] for r in range(3)))
    for r, row in enumerate(rows):
        out_ref[:, r * parts : (r + 1) * parts, :] = jnp.broadcast_to(
            row[None], (out_ref.shape[0], parts, BAND)
        )


def near_merge(messages, members):
    return pl.pallas_call(
        near_merge_kernel,
        out_shape=jax.ShapeDtypeStruct((members, 16, BAND), jnp.float32),
        compiler_params=pltpu.CompilerParams(vmem_limit_bytes=4 * MIB),
        name="near_merge",
    )(messages)


def first_norm(in_ref, gain_ref, bias_ref, scale_col, shift_col):
    parts = gain_ref.shape[0]
    got = in_ref[...]
    count, mean, spread = merge(*(got[:, r * parts : (r + 1) * parts, :] for r in range(3)))
    var = spread / count
    scale = gain_ref[...] * lax.rsqrt(var + EPS)
    for value, col in ((scale, scale_col), (bias_ref[...] - mean * scale, shift_col)):
        for q in range(parts):
            col[q * BAND : (q + 1) * BAND, :] = jnp.broadcast_to(value[q : q + 1, :], (BAND, BAND)).T
    return mean, var


def make_second_kernel(order, pixels, tiles, lanes, last):
    n_in = slots = len(order)
    early = 2 * PIECE

    def kernel(tissue_ref, *refs):
        inputs = refs[:n_in]
        w1_ref, moments_ref, gain_ref, bias_ref = refs[n_in : n_in + 4]
        w2_refs = refs[n_in + 4 : n_in + 8]
        rest = refs[n_in + 8 :]
        if last:
            before_ref, rest = rest[0], rest[1:]
        outs, stats_ref, rest = rest[:8], rest[8], rest[9:]
        if not last:
            mean_ref, var_ref, rest = rest[0], rest[1], rest[2:]
        rows, w2_ref, scale_ref, shift_ref, buffer, sems, out_sems = rest
        core = lax.axis_index("c")
        shift = pl.multiple_of(core * HALF, HALF)

        def load(slot, part):
            start = part * early
            size = lanes - HALF - early if part else early
            return pltpu.make_async_copy(
                inputs[slot].at[pl.ds(start, size), :],
                rows.at[slot, pl.ds(pl.multiple_of(shift + start, 16), size), :],
                sems.at[slot, part],
            )

        for slot in range(slots):
            for part in range(2):
                load(slot, part).start()
            rest_at = pl.multiple_of((1 - core) * (lanes - HALF), HALF)
            rows[slot, pl.ds(rest_at, HALF), :] = jnp.zeros((HALF, rows.shape[2]), rows.dtype)
        for i, ref in enumerate(w2_refs):
            w2_ref[i * ref.shape[0] : (i + 1) * ref.shape[0], :] = ref[...]
        mean, var = first_norm(moments_ref, gain_ref, bias_ref, scale_ref, shift_ref)
        if not last:
            mean_ref[...] = mean
            var_ref[...] = var
        width = outs[0].shape[1]

        def out_copies(slot, part):
            at = part * lanes // 2 // PIECE * PIECE
            size = lanes - at if part else lanes // 2 // PIECE * PIECE
            return [
                pltpu.make_async_copy(
                    buffer.at[i, slot, :, pl.ds(at, size)],
                    outs[i].at[slot, :, pl.ds(at, size)],
                    out_sems.at[i, slot, part],
                )
                for i in range(8)
            ]

        centre = jnp.broadcast_to(before_ref[:, 0:1], (8 * width, BAND)) if last else None
        sums = squares = None
        for slot in range(slots):
            held_here = tissue_of(tissue_ref, *ring_spot(order[slot]), tiles)
            load(slot, 0).wait()
            for at in range(0, lanes, PIECE):
                if at == early:
                    load(slot, 1).wait()
                tile = min(PIECE, lanes - at)
                wide = lambda v: jnp.concatenate([v] * (tile // BAND), axis=1)
                block = rows[slot, at : at + tile, :]
                first = lax.dot_general(
                    w1_ref[...],
                    block,
                    (((1,), (1,)), ((), ())),
                    preferred_element_type=jnp.float32,
                )
                activation = jnp.maximum(
                    (first * wide(scale_ref[...]) + wide(shift_ref[...])).astype(jnp.bfloat16), 0
                )
                second = jnp.dot(w2_ref[...], activation, preferred_element_type=jnp.float32)
                if centre is None:
                    centre = jnp.broadcast_to(
                        jnp.mean(second[:, BAND:], axis=1, keepdims=True), (8 * width, BAND)
                    )
                second = second - wide(centre)
                lane = lax.broadcasted_iota(jnp.int32, (1, tile), 1) + (at - shift)
                held = jnp.zeros((1, tile), jnp.float32)
                for t in range(tiles):
                    inside = (lane >= t * pixels) & (lane < (t + 1) * pixels)
                    held += jnp.where(inside, held_here[t], 0.0)
                kept = second * held
                squared = kept * second
                part = sum(kept[:, i * BAND : (i + 1) * BAND] for i in range(tile // BAND))
                part2 = sum(squared[:, i * BAND : (i + 1) * BAND] for i in range(tile // BAND))
                sums = part if sums is None else sums + part
                squares = part2 if squares is None else squares + part2
                rounded = second.astype(jnp.bfloat16)
                for i in range(8):
                    buffer[i, slot, :, at : at + tile] = rounded[i * width : (i + 1) * width, :]
                if at + tile == lanes // 2 // PIECE * PIECE:
                    for copy in out_copies(slot, 0):
                        copy.start()
            for copy in out_copies(slot, 1):
                copy.start()
        lane = lax.broadcasted_iota(jnp.int32, (8 * width, BAND), 1)
        sums = jnp.sum(sums, axis=1, keepdims=True)
        squares = jnp.sum(squares, axis=1, keepdims=True)
        if last:
            count = sum(
                held for slot in range(RING) for held in tissue_of(tissue_ref, *ring_spot(slot), tiles)
            )
            count = jnp.full((8 * width, 1), count * pixels, jnp.float32)
            mean, spread = local_moments(
                count, before_ref[:, 0:1], before_ref[:, 1:2] + sums, before_ref[:, 2:3] + squares
            )
            message = jnp.where(lane == 0, count, jnp.where(lane == 1, mean, spread)).T[:8, :]
            stats_ref[...] = message
        else:
            stats_ref[...] = jnp.where(lane == 0, centre, jnp.where(lane == 1, sums, squares))
        for slot in range(slots):
            for part in range(2):
                for copy in out_copies(slot, part):
                    copy.wait()

    return kernel


def second_values(tissue, inputs, order, norm, pairs, before, pixels, tiles):
    depth = norm[0].shape[1]
    lanes = pixels * tiles + HALF
    channels = sum(pair.shape[0] for pair in pairs)
    vmem = pl.BlockSpec(memory_space=pltpu.VMEM)
    anywhere = pl.BlockSpec(memory_space=pl.ANY)
    extra = [] if before is None else [before]
    hidden = norm[0].shape[0]
    row = jax.ShapeDtypeStruct((hidden // BAND, BAND), jnp.float32)
    rows_out = [row, row] if before is None else []
    stats = (channels, BAND) if before is None else (8, channels)
    outs = pl.pallas_call(
        make_second_kernel(order, pixels, tiles, lanes, before is not None),
        out_shape=[jax.ShapeDtypeStruct((len(inputs), channels // 8, lanes), jnp.bfloat16)] * 8
        + [jax.ShapeDtypeStruct(stats, jnp.float32), *rows_out],
        in_specs=[pl.BlockSpec(memory_space=pltpu.SMEM)]
        + [pl.BlockSpec(memory_space=pl.ANY)] * len(inputs)
        + [vmem] * (8 + len(extra)),
        out_specs=[anywhere] * 8 + [vmem] * (1 + len(rows_out)),
        scratch_shapes=[
            pltpu.VMEM((len(inputs), lanes, depth), jnp.bfloat16),
            pltpu.VMEM((channels, hidden), jnp.bfloat16),
            pltpu.VMEM((hidden, BAND), jnp.float32),
            pltpu.VMEM((hidden, BAND), jnp.float32),
            pltpu.VMEM((8, len(inputs), channels // 8, lanes), jnp.bfloat16),
            pltpu.SemaphoreType.DMA((len(inputs), 2)),
            pltpu.SemaphoreType.DMA((8, len(inputs), 2)),
        ],
        compiler_params=pltpu.CompilerParams(
            vmem_limit_bytes=(16 + 6 * len(inputs)) * MIB
        ),
        name="second_values",
    )(tissue, *inputs, *norm, *pairs, *extra)
    return outs[:8], *outs[8:]


def stamp_kernel(*refs):
    messages, before_ref, refs = refs[:RING], refs[RING], refs[RING + 1 :]
    blocks, all_ref, buffer, in_sems, out_sems = refs[8:16], refs[16], refs[17], refs[18], refs[19]
    z = lax.axis_index("z")
    for step, ref in enumerate(messages):
        all_ref[(z + RING - step) % RING] = ref[...]
    core = lax.axis_index("c")
    lanes = blocks[0].shape[2]
    spare = pl.ds(pl.multiple_of((1 - core) * (lanes - BAND), BAND), BAND)
    loads = [
        pltpu.make_async_copy(block.at[0, :, spare], buffer.at[i], in_sems.at[i])
        for i, block in enumerate(blocks)
    ]
    stores = [
        pltpu.make_async_copy(buffer.at[i], block.at[0, :, spare], out_sems.at[i])
        for i, block in enumerate(blocks)
    ]
    for copy in loads:
        copy.start()
    got = all_ref[...]
    channels = got.shape[2]
    rows = merge(got[:, 0:1, :], got[:, 1:2, :], got[:, 2:3, :])
    turned = jnp.concatenate([*rows, jnp.zeros((BAND - 3, channels), jnp.float32)], axis=0).T
    lane = lax.broadcasted_iota(jnp.int32, turned.shape, 1) - (1 - core) * HALF
    value = jnp.broadcast_to(before_ref[:, 0:1], turned.shape)
    for q in range(3):
        value = jnp.where(lane % 4 == q, turned[:, q : q + 1], value)
    high = value.astype(jnp.bfloat16).astype(jnp.float32)
    middle = (value - high).astype(jnp.bfloat16).astype(jnp.float32)
    low = value - high - middle
    value = jnp.where(lane < 4, high, jnp.where(lane < 8, middle, low))
    written = (lane >= 0) & (lane < 12)
    width = channels // 8
    for i in range(8):
        loads[i].wait()
        here = slice(i * width, (i + 1) * width)
        buffer[i] = jnp.where(
            written[here], value[here], buffer[i].astype(jnp.float32)
        ).astype(jnp.bfloat16)
        stores[i].start()
    for copy in stores:
        copy.wait()


def stamp(messages, before, blocks):
    vmem = pl.BlockSpec(memory_space=pltpu.VMEM)
    anywhere = pl.BlockSpec(memory_space=pl.ANY)
    width = blocks[0].shape[1]
    return pl.pallas_call(
        stamp_kernel,
        out_shape=[jax.ShapeDtypeStruct(block.shape, block.dtype) for block in blocks],
        in_specs=[vmem] * (RING + 1) + [anywhere] * 8,
        out_specs=[anywhere] * 8,
        scratch_shapes=[
            pltpu.VMEM((RING, *messages[0].shape), jnp.float32),
            pltpu.VMEM((8, width, BAND), jnp.bfloat16),
            pltpu.SemaphoreType.DMA((8,)),
            pltpu.SemaphoreType.DMA((8,)),
        ],
        input_output_aliases={RING + 1 + i: i for i in range(8)},
        compiler_params=pltpu.CompilerParams(vmem_limit_bytes=4 * MIB),
        name="stamp",
    )(*messages, before, *blocks)


def make_last_kernel(lanes, chip_lanes):
    cut = chip_lanes // 2 // BAND * BAND

    def kernel(*refs):
        moved = refs[:16]
        gain_ref, bias_ref, out_ref, mean_ref, var_ref = refs[16:21]
        outbuf, shift_ref, out_sems = refs[21:]
        x, y, core = spot()

        def piece(ring, slot, flip):
            group, row = ((0, 0), (0, 1), (1, 0), (0, 2))[slot]
            return moved[group * 8 + ring * 2 + flip].at[row]

        def store(a, b):
            n = a * RING + b
            chip = ((x + RING - a) % RING) * RING + (y + RING - b) % RING
            return pltpu.make_async_copy(
                outbuf.at[n],
                out_ref.at[:, pl.ds(pl.multiple_of(chip * chip_lanes, BAND), chip_lanes)],
                out_sems.at[n],
            )

        steps = [(a, b) for a in range(RING) for b in range(RING)]
        LAST = 2
        width = moved[0].shape[1]
        lane = lax.broadcasted_iota(jnp.int32, (width, BAND), 1)
        row = lax.broadcasted_iota(jnp.int32, (width, BAND), 0)
        device = place(x, y, core)
        per_row = BAND // width

        def own_channels(ref):
            line = ref[pl.ds(device // per_row, 1), :]
            here = lane == row + (device % per_row) * width
            return jnp.sum(jnp.where(here, line, 0.0), axis=1, keepdims=True)

        gain, bias = own_channels(gain_ref), own_channels(bias_ref)

        def chosen(flip0, flip1):
            return jnp.where(core == 0, flip0.astype(jnp.float32), flip1.astype(jnp.float32))

        ends = (slice(lanes - BAND, lanes), slice(0, BAND))
        notes = []
        for i in range(2):
            for k in range(RING):
                both = [piece(k, LAST, i), piece(k, LAST, 1 - i)]
                notes.append(chosen(*(ref[:, ends[i]] for ref in both)))

        def read(q):
            out = []
            for n, note in enumerate(notes):
                at = q + (HALF if n < RING else 0)
                out.append(note[:, at : at + 1] + note[:, at + 4 : at + 5] + note[:, at + 8 : at + 9])
            return jnp.stack(out)

        count, mean, spread = merge(read(0), read(1), read(2))
        var = spread / count
        centre = read(3)
        slope = gain * lax.rsqrt(var + EPS)
        for n in range(2 * RING):
            shift_ref[n] = jnp.broadcast_to((centre[n] - mean) * slope + bias, (width, BAND))
        scale = jnp.broadcast_to(slope, (width, BAND))
        for value, ref in ((mean, mean_ref), (var, var_ref)):
            line = jnp.sum(jnp.where(lane == row, value, 0.0), axis=0, keepdims=True)
            ref[...] = line[:, :width]

        def finish(values, shift):
            wide = lambda v: jnp.concatenate([v] * (values.shape[1] // BAND), axis=1)
            return values.astype(jnp.float32) * wide(scale) + wide(shift)

        for c in range(2):

            @pl.when(core == c)
            def _():
                for a, b in steps:
                    n = a * RING + b
                    left_shift = shift_ref[b]
                    right_shift = shift_ref[RING + a]
                    left = piece(b, a, c)
                    right = piece(a, b, 1 - c)
                    middle = jnp.where(
                        lane < HALF,
                        finish(left[:, cut : cut + BAND], left_shift),
                        finish(right[:, :BAND], right_shift),
                    )
                    for at, value in (
                        (0, finish(left[:, :cut], left_shift)),
                        (cut, middle),
                        (cut + BAND, finish(right[:, BAND:], right_shift)),
                    ):
                        outbuf[n, :, at : at + value.shape[1]] = jnp.maximum(
                            value.astype(jnp.bfloat16), 0
                        )
                    store(a, b).start()

        for a, b in steps:
            store(a, b).wait()

    return kernel


def last_pass(moved, gain, bias, chip_lanes):
    _, width, lanes = moved[0].shape
    vmem = pl.BlockSpec(memory_space=pltpu.VMEM)
    hbm = pl.BlockSpec(memory_space=pl.ANY)
    chips = RING * RING
    stat = jax.ShapeDtypeStruct((1, width), jnp.float32)
    return pl.pallas_call(
        make_last_kernel(lanes, chip_lanes),
        out_shape=[jax.ShapeDtypeStruct((width, chips * chip_lanes), jnp.bfloat16), stat, stat],
        in_specs=[vmem] * 18,
        out_specs=[hbm, vmem, vmem],
        scratch_shapes=[
            pltpu.VMEM((chips, width, chip_lanes), jnp.bfloat16),
            pltpu.VMEM((8, width, BAND), jnp.float32),
            pltpu.SemaphoreType.DMA((chips,)),
        ],
        compiler_params=pltpu.CompilerParams(vmem_limit_bytes=24 * MIB),
        name="last_pass",
    )(*moved, gain.reshape(-1, BAND), bias.reshape(-1, BAND))


def trade(messages, axes):
    return lax.all_to_all(messages, axes, split_axis=0, concat_axis=0, tiled=True)


ROUTES = [(step, flip) for step in range(RING) for flip in range(2)]


def send(blocks):
    out = []
    for route, block in zip(ROUTES, blocks):
        if route != (0, 0):
            block = exchange_step(block, *route)
        out.append(block)
    return out


def shards(
    features, tissue, first_weight, first_gain, first_bias, second_weight, second_gain, second_bias
):
    tiles, pixels, depth = features.shape[1:]
    rows = features.reshape(tiles * pixels, depth)
    row_tissue = tissue[0]
    own = second_weight.T
    mate = lax.ppermute(own, "c", [(0, 1), (1, 0)])
    ahead = gather_step(rows, 1)
    behind = gather_step(rows, 3)
    messages, w1t, pair = first_sums(
        row_tissue, features[0], first_weight, own, mate, 2 * RING
    )
    messages = trade(messages, ("z", "c"))
    after, before = exchange_step(pair, 3, 0), exchange_step(pair, 1, 0)
    messages = near_merge(messages, RING * RING)
    messages = trade(messages, ("x", "y"))
    across = exchange_step(pair, 2, 0)
    far = gather_step(rows, 2)
    pairs = [pair, after, across, before]
    norm = [w1t, messages] + [v.reshape(-1, BAND) for v in (first_gain, first_bias)]
    near, sums, first_mean, first_var = second_values(
        row_tissue, [rows, ahead, behind], (0, 1, 3), norm, pairs, None, pixels, tiles
    )
    moved = send(near)
    rest, messages = second_values(row_tissue, [far], (2,), norm, pairs, sums, pixels, tiles)
    messages = [messages] + [
        lax.ppermute(messages, "z", [(i, (i + step) % RING) for i in range(RING)])
        for step in range(1, RING)
    ]
    rest = stamp(messages, sums, rest)
    moved += send(rest)
    output, second_mean, second_var = last_pass(moved, second_gain, second_bias, 2 * tiles * pixels)
    return (
        output[None],
        first_mean.reshape(-1),
        first_var.reshape(-1),
        second_mean[0],
        second_var[0],
    )


def solution(mesh):
    fine = Mesh(mesh.devices.reshape(RING, RING, RING, 2), EVERY)
    in_specs = (
        P("z", PLANE, None, None),
        P("z", None),
        P(),
        P(),
        P(),
        P(None, PLANE),
        P(),
        P(),
    )
    out_specs = (P("z", PLANE, None), P(), P(), P(PLANE), P(PLANE))
    return jax.shard_map(
        shards, mesh=fine, in_specs=in_specs, out_specs=out_specs, check_vma=False
    )
```

```python
import jax
import jax.numpy as jnp
from jax import lax
from jax.experimental import pallas as pl
from jax.experimental.pallas import tpu as pltpu
from jax.sharding import Mesh
from jax.sharding import PartitionSpec as P


EPS = 1e-05
EVERY = ("z", "x", "y", "c")
PLANE = ("x", "y", "c")
RING = 4
MIB = 1 << 20
GRANT = 24
TURNS = (1, 0, 2, 3)
BAND = 128
HALF = BAND // 2
PIECE = 512


def place(x, y, c):
    return ((x % RING) * RING + y % RING) * 2 + c


def along(step, core0_axis, flip):
    pairs = []
    for x in range(RING):
        for y in range(RING):
            for c in range(2):
                on_x = (core0_axis == "x") == (c == 0)
                there = (x + step, y) if on_x else (x, y + step)
                pairs.append((place(x, y, c), place(*there, c ^ flip)))
    return pairs


def gather_step(values, step):
    return lax.ppermute(values, PLANE, along(step, "x", 0))


def exchange_step(values, step, flip):
    return lax.ppermute(values, PLANE, along(step, "y", flip))


def spot():
    return tuple(lax.axis_index(axis) for axis in PLANE)


def tissue_of(tissue_ref, chip_x, chip_y, core, tiles):
    base = place(chip_x, chip_y, core) * tiles
    return [tissue_ref[base + t].astype(jnp.float32) for t in range(tiles)]


def ring_spot(slot):
    x, y, c = spot()
    along_x, along_y = (1 - c) * slot, c * slot
    return (x + RING - along_x) % RING, (y + RING - along_y) % RING, c


def merge(counts, means, squares):
    total = jnp.sum(counts, axis=0)
    centre = means[0]
    mean_val = centre + jnp.sum(counts * (means - centre), axis=0) / jnp.maximum(total, 1.0)
    spread = jnp.sum(squares + counts * (means - mean_val) ** 2, axis=0)
    return total, mean_val, spread


def local_moments(count, centre, sums, squares):
    safe = jnp.maximum(count, 1.0)
    return centre + sums / safe, squares - sums * sums / safe


def first_kernel(
    tissue_ref, rows_ref, weight_ref, own_ref, mate_ref, out_ref, pair_ref, buffer, sems
):
    tiles, pixels, _ = rows_ref.shape
    width = weight_ref.shape[1]
    loads = [
        pltpu.make_async_copy(rows_ref.at[t], buffer.at[t], sems.at[t]) for t in range(tiles)
    ]
    for copy in loads:
        copy.start()
    half = own_ref.shape[0]
    pair_ref[:half, :] = own_ref[...]
    pair_ref[half:, :] = mate_ref[...]
    chunk = pixels // 7
    centre = None
    sums = squares = count = 0.0
    for t, held in enumerate(tissue_of(tissue_ref, *spot(), tiles)):
        loads[t].wait()
        part_sums = jnp.zeros((8, width), jnp.float32)
        part_squares = jnp.zeros((8, width), jnp.float32)
        for i in range(7):
            part = jnp.dot(
                buffer[t, i * chunk : (i + 1) * chunk, :],
                weight_ref[...],
                preferred_element_type=jnp.float32,
            )
            if centre is None:
                centre = jnp.mean(part, axis=0, keepdims=True)
            centred = (part - centre).reshape(chunk // 8, 8, width)
            part_sums += jnp.sum(centred, axis=0)
            part_squares += jnp.sum(centred * centred, axis=0)
        sums += held * part_sums
        squares += held * part_squares
        count += held * pixels
    count = jnp.full((1, width), count, jnp.float32)
    mean, spread = local_moments(
        count,
        centre,
        jnp.sum(sums, axis=0, keepdims=True),
        jnp.sum(squares, axis=0, keepdims=True),
    )
    parts = width // BAND
    for r, row in enumerate((count, mean, spread)):
        for q in range(parts):
            out_ref[:, r * parts + q, :] = jnp.broadcast_to(
                row[:, q * BAND : (q + 1) * BAND], (out_ref.shape[0], BAND)
            )


def first_sums(tissue, rows, weight, own, mate, members):
    vmem = pl.BlockSpec(memory_space=pltpu.VMEM)
    return pl.pallas_call(
        first_kernel,
        out_shape=[
            jax.ShapeDtypeStruct((members, 16, BAND), jnp.float32),
            jax.ShapeDtypeStruct((2 * own.shape[0], own.shape[1]), jnp.bfloat16),
        ],
        in_specs=[
            pl.BlockSpec(memory_space=pltpu.SMEM),
            pl.BlockSpec(memory_space=pltpu.HBM),
            vmem,
            vmem,
            vmem,
        ],
        out_specs=[vmem] * 2,
        scratch_shapes=[
            pltpu.VMEM(rows.shape, rows.dtype),
            pltpu.SemaphoreType.DMA((rows.shape[0],)),
        ],
        name="first_sums",
    )(tissue, rows, weight, own, mate)


def near_merge_kernel(in_ref, out_ref):
    parts = 4
    got = in_ref[...]
    rows = merge(*(got[:, r * parts : (r + 1) * parts, :] for r in range(3)))
    for r, row in enumerate(rows):
        out_ref[:, r * parts : (r + 1) * parts, :] = jnp.broadcast_to(
            row[None], (out_ref.shape[0], parts, BAND)
        )


def near_merge(messages, members):
    return pl.pallas_call(
        near_merge_kernel,
        out_shape=jax.ShapeDtypeStruct((members, 16, BAND), jnp.float32),
        compiler_params=pltpu.CompilerParams(vmem_limit_bytes=4 * MIB),
        name="near_merge",
    )(messages)


def first_norm(in_ref, gain_ref, bias_ref, scale_col, shift_col):
    parts = gain_ref.shape[0]
    got = in_ref[...]
    count, mean, spread = merge(*(got[:, r * parts : (r + 1) * parts, :] for r in range(3)))
    var = spread / count
    scale = gain_ref[...] * lax.rsqrt(var + EPS)
    for value, col in ((scale, scale_col), (bias_ref[...] - mean * scale, shift_col)):
        for q in range(parts):
            col[q * BAND : (q + 1) * BAND, :] = jnp.broadcast_to(value[q : q + 1, :], (BAND, BAND)).T
    return mean, var


def make_second_kernel(order, pixels, tiles, lanes, n_pairs, n_before, given, kept):
    slots = len(order)

    def kernel(tissue_ref, *refs):
        refs = list(refs)
        take = lambda n: [refs.pop(0) for _ in range(n)]
        if given:
            (act_ref,) = take(1)
        else:
            inputs = take(slots)
            w1_ref, moments_ref, gain_ref, bias_ref = take(4)
        w2_refs, before_refs = take(n_pairs), take(n_before)
        outs, (stats_ref,) = take(2 * n_pairs), take(1)
        if kept:
            mean_ref, var_ref, act_ref = take(3)
        (w2_ref,) = take(1)
        core = lax.axis_index("c")
        shift = pl.multiple_of(core * HALF, HALF)
        for i, ref in enumerate(w2_refs):
            w2_ref[i * ref.shape[0] : (i + 1) * ref.shape[0], :] = ref[...]
        if not given:
            scale_ref, shift_ref, head_ref, tail_ref, turned_ref = take(5)
            turned_ref[...] = w1_ref[...].T
            mean, var = first_norm(moments_ref, gain_ref, bias_ref, scale_ref, shift_ref)
            if kept:
                mean_ref[...] = mean
                var_ref[...] = var
            end = lanes - HALF
            rest = end - (lanes - BAND)
            zeros = jnp.zeros((HALF, head_ref.shape[2]), head_ref.dtype)
            for slot, rows in enumerate(inputs):

                @pl.when(core == 0)
                def _():
                    head_ref[slot] = rows[:PIECE, :]
                    tail_ref[slot, :rest] = rows[end - rest :, :]
                    tail_ref[slot, rest:] = zeros

                @pl.when(core == 1)
                def _():
                    head_ref[slot, :HALF] = zeros
                    head_ref[slot, HALF:] = rows[: PIECE - HALF, :]
                    tail_ref[slot] = rows[end - BAND :, :]

        width = outs[0].shape[1]
        channels = 2 * n_pairs * width
        centre = None
        if n_before:
            centre = jnp.concatenate([ref[:, 0:1] for ref in before_refs], axis=0)
            centre = jnp.broadcast_to(centre, (channels, BAND))
        sums = squares = None
        for slot in range(slots):
            held_here = tissue_of(tissue_ref, *ring_spot(order[slot]), tiles)
            for at in range(0, lanes, PIECE):
                tile = min(PIECE, lanes - at)
                wide = lambda v: jnp.concatenate([v] * (tile // BAND), axis=1)
                if given:
                    activation = act_ref[slot, :, at : at + tile]
                else:
                    if at == 0:
                        block = head_ref[slot]
                    elif tile == PIECE:
                        block = inputs[slot][pl.ds(pl.multiple_of(at - shift, HALF), tile), :]
                    else:
                        block = tail_ref[slot]
                    first = lax.dot_general(
                        turned_ref[...],
                        block,
                        (((1,), (1,)), ((), ())),
                        preferred_element_type=jnp.float32,
                    )
                    activation = jnp.maximum(
                        (first * wide(scale_ref[...]) + wide(shift_ref[...])).astype(jnp.bfloat16), 0
                    )
                    if kept:
                        act_ref[slot, :, at : at + tile] = activation
                second = jnp.dot(w2_ref[...], activation, preferred_element_type=jnp.float32)
                if centre is None:
                    centre = jnp.broadcast_to(
                        jnp.mean(second[:, BAND:], axis=1, keepdims=True), (channels, BAND)
                    )
                second = second - wide(centre)
                lane = lax.broadcasted_iota(jnp.int32, (1, tile), 1) + (at - shift)
                held = jnp.zeros((1, tile), jnp.float32)
                for t in range(tiles):
                    inside = (lane >= t * pixels) & (lane < (t + 1) * pixels)
                    held += jnp.where(inside, held_here[t], 0.0)
                keep = second * held
                squared = keep * second
                part = sum(keep[:, i * BAND : (i + 1) * BAND] for i in range(tile // BAND))
                part2 = sum(squared[:, i * BAND : (i + 1) * BAND] for i in range(tile // BAND))
                sums = part if sums is None else sums + part
                squares = part2 if squares is None else squares + part2
                rounded = second.astype(jnp.bfloat16)
                for i, out in enumerate(outs):
                    out[slot, :, at : at + tile] = rounded[i * width : (i + 1) * width, :]
        lane = lax.broadcasted_iota(jnp.int32, (channels, BAND), 1)
        sums = jnp.sum(sums, axis=1, keepdims=True)
        squares = jnp.sum(squares, axis=1, keepdims=True)
        if n_before:
            count = sum(
                held for slot in range(RING) for held in tissue_of(tissue_ref, *ring_spot(slot), tiles)
            )
            count = jnp.full((channels, 1), count * pixels, jnp.float32)
            so_far = lambda q: jnp.concatenate([ref[:, q : q + 1] for ref in before_refs], axis=0)
            mean, spread = local_moments(count, so_far(0), so_far(1) + sums, so_far(2) + squares)
            stats_ref[...] = jnp.where(lane == 0, count, jnp.where(lane == 1, mean, spread)).T[:8, :]
        else:
            stats_ref[...] = jnp.where(lane == 0, centre, jnp.where(lane == 1, sums, squares))

    return kernel


def second_values(tissue, rows, order, norm, pairs, before, pixels, tiles, act=None, keep=False):
    vmem = pl.BlockSpec(memory_space=pltpu.VMEM)
    given = act is not None
    slots = len(order)
    depth, hidden = norm[0].shape
    lanes = pixels * tiles + HALF
    channels = sum(pair.shape[0] for pair in pairs)
    width = channels // (2 * len(pairs))
    stat = jax.ShapeDtypeStruct((8, channels) if before else (channels, BAND), jnp.float32)
    block = jax.ShapeDtypeStruct((slots, width, lanes), jnp.bfloat16)
    out_shape = [block] * (2 * len(pairs)) + [stat]
    if keep:
        row = jax.ShapeDtypeStruct((hidden // BAND, BAND), jnp.float32)
        out_shape += [row, row, jax.ShapeDtypeStruct((slots, hidden, lanes), jnp.bfloat16)]
    scratch = [pltpu.VMEM((channels, hidden), jnp.bfloat16)]
    if not given:
        scratch += [
            pltpu.VMEM((hidden, BAND), jnp.float32),
            pltpu.VMEM((hidden, BAND), jnp.float32),
            pltpu.VMEM((slots, PIECE, depth), jnp.bfloat16),
            pltpu.VMEM((slots, BAND, depth), jnp.bfloat16),
            pltpu.VMEM((hidden, depth), jnp.bfloat16),
        ]
    operands = [act] if given else [*rows, *norm]
    operands += [*pairs, *before]
    kernel = make_second_kernel(
        order, pixels, tiles, lanes, len(pairs), len(before), given, keep
    )
    outs = pl.pallas_call(
        kernel,
        out_shape=out_shape,
        in_specs=[pl.BlockSpec(memory_space=pltpu.SMEM)] + [vmem] * len(operands),
        out_specs=[vmem] * len(out_shape),
        scratch_shapes=scratch,
        compiler_params=pltpu.CompilerParams(vmem_limit_bytes=GRANT * MIB),
        name="second_values",
    )(tissue, *operands)
    return outs[: 2 * len(pairs)], *outs[2 * len(pairs) :]


def stamp_kernel(*refs):
    messages, before_refs, refs = refs[:RING], refs[RING : RING + 2], refs[RING + 2 :]
    blocks, all_ref, buffer, in_sems, out_sems = refs[8:16], refs[16], refs[17], refs[18], refs[19]
    z = lax.axis_index("z")
    for step, ref in enumerate(messages):
        all_ref[(z + RING - step) % RING] = ref[...]
    core = lax.axis_index("c")
    lanes = blocks[0].shape[2]
    spare = pl.ds(pl.multiple_of((1 - core) * (lanes - BAND), BAND), BAND)
    loads = [
        pltpu.make_async_copy(block.at[0, :, spare], buffer.at[i], in_sems.at[i])
        for i, block in enumerate(blocks)
    ]
    stores = [
        pltpu.make_async_copy(buffer.at[i], block.at[0, :, spare], out_sems.at[i])
        for i, block in enumerate(blocks)
    ]
    for copy in loads:
        copy.start()
    got = all_ref[...]
    channels = got.shape[2]
    rows = merge(got[:, 0:1, :], got[:, 1:2, :], got[:, 2:3, :])
    turned = jnp.concatenate([*rows, jnp.zeros((BAND - 3, channels), jnp.float32)], axis=0).T
    lane = lax.broadcasted_iota(jnp.int32, turned.shape, 1) - (1 - core) * HALF
    centre = jnp.concatenate([ref[:, 0:1] for ref in before_refs], axis=0)
    value = jnp.broadcast_to(centre, turned.shape)
    for q in range(3):
        value = jnp.where(lane % 4 == q, turned[:, q : q + 1], value)
    high = value.astype(jnp.bfloat16).astype(jnp.float32)
    middle = (value - high).astype(jnp.bfloat16).astype(jnp.float32)
    low = value - high - middle
    value = jnp.where(lane < 4, high, jnp.where(lane < 8, middle, low))
    written = (lane >= 0) & (lane < 12)
    width = channels // 8
    for i in range(8):
        loads[i].wait()
        here = slice(i * width, (i + 1) * width)
        buffer[i] = jnp.where(
            written[here], value[here], buffer[i].astype(jnp.float32)
        ).astype(jnp.bfloat16)
        stores[i].start()
    for copy in stores:
        copy.wait()


def stamp(messages, before, blocks):
    vmem = pl.BlockSpec(memory_space=pltpu.VMEM)
    anywhere = pl.BlockSpec(memory_space=pl.ANY)
    width = blocks[0].shape[1]
    return pl.pallas_call(
        stamp_kernel,
        out_shape=[jax.ShapeDtypeStruct(block.shape, block.dtype) for block in blocks],
        in_specs=[vmem] * (RING + 2) + [anywhere] * 8,
        out_specs=[anywhere] * 8,
        scratch_shapes=[
            pltpu.VMEM((RING, *messages[0].shape), jnp.float32),
            pltpu.VMEM((8, width, BAND), jnp.bfloat16),
            pltpu.SemaphoreType.DMA((8,)),
            pltpu.SemaphoreType.DMA((8,)),
        ],
        input_output_aliases={RING + 2 + i: i for i in range(8)},
        compiler_params=pltpu.CompilerParams(vmem_limit_bytes=4 * MIB),
        name="stamp",
    )(*messages, *before, *blocks)


def make_last_kernel(lanes, chip_lanes):
    cut = chip_lanes // 2 // BAND * BAND

    def kernel(*refs):
        moved = refs[:16]
        gain_ref, bias_ref, out_ref, mean_ref, var_ref = refs[16:21]
        outbuf, shift_ref, out_sems = refs[21:]
        x, y, core = spot()

        def piece(ring, slot, flip):
            group, row = ((0, 0), (0, 1), (1, 0), (0, 2))[slot]
            return moved[group * 8 + ring * 2 + flip].at[row]

        def store(a, b):
            n = a * RING + b
            chip = ((x + RING - a) % RING) * RING + (y + RING - b) % RING
            return pltpu.make_async_copy(
                outbuf.at[n],
                out_ref.at[:, pl.ds(pl.multiple_of(chip * chip_lanes, BAND), chip_lanes)],
                out_sems.at[n],
            )

        steps = [(a, b) for a in range(RING) for b in range(RING)]
        LAST = 2
        width = moved[0].shape[1]
        lane = lax.broadcasted_iota(jnp.int32, (width, BAND), 1)
        row = lax.broadcasted_iota(jnp.int32, (width, BAND), 0)
        device = place(x, y, core)
        per_row = BAND // width

        def own_channels(ref):
            line = ref[pl.ds(device // per_row, 1), :]
            here = lane == row + (device % per_row) * width
            return jnp.sum(jnp.where(here, line, 0.0), axis=1, keepdims=True)

        gain, bias = own_channels(gain_ref), own_channels(bias_ref)

        def chosen(flip0, flip1):
            return jnp.where(core == 0, flip0.astype(jnp.float32), flip1.astype(jnp.float32))

        ends = (slice(lanes - BAND, lanes), slice(0, BAND))
        notes = []
        for i in range(2):
            for k in range(RING):
                both = [piece(k, LAST, i), piece(k, LAST, 1 - i)]
                notes.append(chosen(*(ref[:, ends[i]] for ref in both)))

        def read(q):
            out = []
            for n, note in enumerate(notes):
                at = q + (HALF if n < RING else 0)
                out.append(note[:, at : at + 1] + note[:, at + 4 : at + 5] + note[:, at + 8 : at + 9])
            return jnp.stack(out)

        count, mean, spread = merge(read(0), read(1), read(2))
        var = spread / count
        centre = read(3)
        slope = gain * lax.rsqrt(var + EPS)
        for n in range(2 * RING):
            shift_ref[n] = jnp.broadcast_to((centre[n] - mean) * slope + bias, (width, BAND))
        scale = jnp.broadcast_to(slope, (width, BAND))
        for value, ref in ((mean, mean_ref), (var, var_ref)):
            line = jnp.sum(jnp.where(lane == row, value, 0.0), axis=0, keepdims=True)
            ref[...] = line[:, :width]

        def finish(values, shift):
            wide = lambda v: jnp.concatenate([v] * (values.shape[1] // BAND), axis=1)
            return values.astype(jnp.float32) * wide(scale) + wide(shift)

        for c in range(2):

            @pl.when(core == c)
            def _():
                for a, b in steps:
                    n = a * RING + b
                    left_shift = shift_ref[b]
                    right_shift = shift_ref[RING + a]
                    left = piece(b, a, c)
                    right = piece(a, b, 1 - c)
                    middle = jnp.where(
                        lane < HALF,
                        finish(left[:, cut : cut + BAND], left_shift),
                        finish(right[:, :BAND], right_shift),
                    )
                    for at, value in (
                        (0, finish(left[:, :cut], left_shift)),
                        (cut, middle),
                        (cut + BAND, finish(right[:, BAND:], right_shift)),
                    ):
                        outbuf[n, :, at : at + value.shape[1]] = jnp.maximum(
                            value.astype(jnp.bfloat16), 0
                        )
                    store(a, b).start()

        for a, b in steps:
            store(a, b).wait()

    return kernel


def last_pass(moved, gain, bias, chip_lanes):
    _, width, lanes = moved[0].shape
    vmem = pl.BlockSpec(memory_space=pltpu.VMEM)
    hbm = pl.BlockSpec(memory_space=pl.ANY)
    chips = RING * RING
    stat = jax.ShapeDtypeStruct((1, width), jnp.float32)
    return pl.pallas_call(
        make_last_kernel(lanes, chip_lanes),
        out_shape=[jax.ShapeDtypeStruct((width, chips * chip_lanes), jnp.bfloat16), stat, stat],
        in_specs=[vmem] * 18,
        out_specs=[hbm, vmem, vmem],
        scratch_shapes=[
            pltpu.VMEM((chips, width, chip_lanes), jnp.bfloat16),
            pltpu.VMEM((8, width, BAND), jnp.float32),
            pltpu.SemaphoreType.DMA((chips,)),
        ],
        compiler_params=pltpu.CompilerParams(vmem_limit_bytes=24 * MIB),
        name="last_pass",
    )(*moved, gain.reshape(-1, BAND), bias.reshape(-1, BAND))


def trade(messages, axes):
    return lax.all_to_all(messages, axes, split_axis=0, concat_axis=0, tiled=True)


ROUTES = [(step, flip) for step in range(RING) for flip in range(2)]


def send(blocks, steps):
    out = {}
    routes = [(step, flip) for step in steps for flip in range(2)]
    for route, block in zip(routes, blocks):
        if route != (0, 0):
            block = exchange_step(block, *route)
        out[route] = block
    return out


def shards(
    features, tissue, first_weight, first_gain, first_bias, second_weight, second_gain, second_bias
):
    tiles, pixels, depth = features.shape[1:]
    rows = features.reshape(tiles * pixels, depth)
    row_tissue = tissue[0]
    own = second_weight.T
    mate = lax.ppermute(own, "c", [(0, 1), (1, 0)])
    ahead = gather_step(rows, 1)
    behind = gather_step(rows, 3)
    messages, pair = first_sums(
        row_tissue, features[0], first_weight, own, mate, 2 * RING
    )
    messages = trade(messages, ("z", "c"))
    after, before = exchange_step(pair, 3, 0), exchange_step(pair, 1, 0)
    messages = near_merge(messages, RING * RING)
    messages = trade(messages, ("x", "y"))
    across = exchange_step(pair, 2, 0)
    far = gather_step(rows, 2)
    pairs = dict(zip(range(RING), (pair, after, across, before)))
    norm = [first_weight, messages] + [v.reshape(-1, BAND) for v in (first_gain, first_bias)]
    near_slots = (row_tissue, [rows, ahead, behind], (0, 1, 3), norm)
    moved = {}
    blocks, sums, first_mean, first_var, act = second_values(
        *near_slots, [pairs[TURNS[0]]], [], pixels, tiles, keep=True
    )
    moved.update(send(blocks, TURNS[:1]))
    blocks, more = second_values(
        *near_slots, [pairs[k] for k in TURNS[1:]], [], pixels, tiles, act=act
    )
    moved.update(send(blocks, TURNS[1:]))
    rest, messages = second_values(
        row_tissue, [far], (2,), norm, [pairs[k] for k in TURNS], [sums, more], pixels, tiles
    )
    messages = [messages] + [
        lax.ppermute(messages, "z", [(i, (i + step) % RING) for i in range(RING)])
        for step in range(1, RING)
    ]
    rest = send(stamp(messages, [sums, more], rest), TURNS)
    moved = [moved[route] for route in ROUTES] + [rest[route] for route in ROUTES]
    output, second_mean, second_var = last_pass(moved, second_gain, second_bias, 2 * tiles * pixels)
    return (
        output[None],
        first_mean.reshape(-1),
        first_var.reshape(-1),
        second_mean[0],
        second_var[0],
    )


def solution(mesh):
    fine = Mesh(mesh.devices.reshape(RING, RING, RING, 2), EVERY)
    in_specs = (
        P("z", PLANE, None, None),
        P("z", None),
        P(),
        P(),
        P(),
        P(None, PLANE),
        P(),
        P(),
    )
    out_specs = (P("z", PLANE, None), P(), P(), P(PLANE), P(PLANE))
    return jax.shard_map(
        shards, mesh=fine, in_specs=in_specs, out_specs=out_specs, check_vma=False
    )
```
